768 devices in a mesh: row: 32 (over y, x), col: 24 (over z, core).
Axes of the slice: x: 4, y: 8, z: 12, core: 2. Of those that a mesh axis runs over, the one named last changes fastest.
Arguments:
- covariance: float32 [3, 32, 4, 24, 128, 128], P(None, 'row', None, 'col'), may hold values from -2 to 2, as said below
- tile_mask: int32 [96, 96], replicated, may hold values from 0 to 1, as said below
Outputs:
- updated: bfloat16 [3, 32, 4, 24, 128, 128], P(None, 'row', None, 'col')
The draws below stay inside these ranges and needn't reach their ends.
Inputs may be any that keep to these rules, and one draw needn't show every extreme that they name: `covariance`: symmetric; the masked leading block of order 512 is positive definite. `tile_mask`: symmetric; tiles on the diagonal and next to it, and tiles whose row and column both lie among the first 4 tile rows, are all ones.
All inputs are finite; a program needn't handle non-finite values.
Results may differ from the reference program's by a relative error of at most 0.001.
Values sent between devices are 32-bit elements; how exact they have to be, the bound alone decides.
A program may use at most 32 MiB of HBM per device.

```python
import jax
import jax.numpy as jnp
from jax import lax

B = 128
TPP = 2
PANELS = 2
TR = 3
W = 256
LEAD = 512
NT = 96
TC = 4
NORD = 12288
N_ROW = 32
N_COL = 24


def draw_covariance(key, part):
    base = jax.random.fold_in(key, 11)
    key_sym, key_sign, key_diag = jax.random.split(base, 3)
    key_points = jax.random.fold_in(base, 37)
    entries = jax.random.uniform(key_sym, (NORD, NORD), jnp.float32, -1.0, 1.0)
    symmetric = 0.5 * (entries + entries.T)
    position = jnp.arange(NORD)
    signs = jnp.where(jax.random.uniform(key_sign, (NORD,)) < 0.5, -1.0, 1.0)
    diag_values = 1.5 + 0.5 * jax.random.uniform(key_diag, (NORD,))
    row_lead = position[:, None] < LEAD
    col_lead = position[None, :] < LEAD
    scales = jnp.ones((NORD,), jnp.float32)
    trail_part = symmetric
    far_sign = jnp.where(row_lead, signs[None, :], signs[:, None])
    far_scale = jnp.where(row_lead, scales[None, :], scales[:, None])
    panel_part = 0.08 * (0.45 * far_sign + symmetric) * far_scale
    points = jax.random.uniform(key_points, (LEAD, 3), jnp.float32, 0.0, 1.0)
    gaps = points[:, None, :] - points[None, :, :]
    distance = jnp.sqrt(gaps[:, :, 0] * gaps[:, :, 0] + gaps[:, :, 1] * gaps[:, :, 1] + gaps[:, :, 2] * gaps[:, :, 2])
    lead_block = 0.05 * jnp.exp(-distance / 0.25) + 0.025 * symmetric[:LEAD, :LEAD]
    lead_part = jnp.pad(lead_block, ((0, NORD - LEAD), (0, NORD - LEAD)))
    both_lead = jnp.logical_and(row_lead, col_lead)
    one_lead = jnp.logical_or(row_lead, col_lead)
    matrix = jnp.where(both_lead, lead_part, jnp.where(one_lead, panel_part, trail_part))
    matrix = jnp.where(position[:, None] == position[None, :], diag_values[:, None], matrix)
    tiled = jnp.transpose(matrix.reshape(NT, B, NT, B), (0, 2, 1, 3))
    return tiled.reshape(TR, N_ROW, TC, N_COL, B, B)


def draw_tile_mask(key, part):
    base = jax.random.fold_in(key, 23)
    key_level, key_roll = jax.random.split(base)
    level = jax.random.randint(key_level, (NT,), 0, 5)
    rolled = jax.random.randint(key_roll, (NT, NT), 0, 1000)
    threshold = 30 + 25 * (level[:, None] + level[None, :])
    chosen = rolled < threshold
    chosen = jnp.logical_or(chosen, chosen.T)
    tile_index = jnp.arange(NT)
    banded = jnp.abs(tile_index[:, None] - tile_index[None, :]) <= 1
    lead_tiles = PANELS * TPP
    lead_square = jnp.logical_and(tile_index[:, None] < lead_tiles, tile_index[None, :] < lead_tiles)
    return jnp.logical_or(jnp.logical_or(chosen, banded), lead_square).astype(jnp.int32)


def setup_inputs(seed: int = 0) -> dict:
    splits = jax.random.split(jax.random.key(seed), 3)
    covariance = draw_covariance(jax.random.fold_in(splits[2], 71), 0)
    tile_mask = draw_tile_mask(jax.random.fold_in(splits[2], 71), 0)
    return {"covariance": covariance, "tile_mask": tile_mask}


def assemble(covariance, tile_mask):
    tiles = covariance.reshape(NT, NT, B, B) * tile_mask.astype(jnp.float32)[:, :, None, None]
    return jnp.transpose(tiles, (0, 2, 1, 3)).reshape(NORD, NORD)

def reference(covariance, tile_mask):
    matrix = assemble(covariance, tile_mask)
    columns = []
    for panel_index in range(PANELS):
        diag_block = matrix[:W, :W]
        lower_factor = jnp.linalg.cholesky(diag_block)
        below = lax.linalg.triangular_solve(lower_factor, matrix[W:, :W], left_side=False, lower=True, transpose_a=True)
        above_zero = jnp.zeros((panel_index * W, W), jnp.float32)
        columns.append(jnp.concatenate([above_zero, lower_factor, below], axis=0))
        matrix = matrix[W:, W:] - jnp.dot(below.astype(jnp.float32), below.T.astype(jnp.float32), precision=lax.Precision.HIGHEST, preferred_element_type=jnp.float32)
    factor_part = jnp.concatenate(columns, axis=1)
    top_rows = jnp.concatenate([factor_part[:LEAD], jnp.zeros((LEAD, NORD - LEAD), jnp.float32)], axis=1)
    bottom_rows = jnp.concatenate([factor_part[LEAD:], matrix], axis=1)
    natural = jnp.concatenate([top_rows, bottom_rows], axis=0)
    tiled = jnp.transpose(natural.reshape(NT, B, NT, B), (0, 2, 1, 3))
    return tiled.reshape(TR, N_ROW, TC, N_COL, B, B).astype(jnp.bfloat16)
```

```python
import functools

import jax
import jax.numpy as jnp
from jax import lax
from jax.experimental import pallas as pl
from jax.experimental.pallas import tpu as pltpu
from jax.sharding import PartitionSpec as P

MESH = pl.DeviceIdType.MESH
f32 = jnp.float32
NN = (((1,), (0,)), ((), ()))
NT = (((1,), (1,)), ((), ()))
TN = (((0,), (0,)), ((), ()))
NX = 4
NY = 8
NZ = 12
LEAD_TILES = 4
SEND_SEMS = 120


def dot(a, b, dims=NN):
    return lax.dot_general(
        a, b, dims, precision=lax.Precision.HIGHEST, preferred_element_type=f32
    )


class Spread:
    def __init__(self, lead, rows, cols, recv, sent):
        self.lead, self.rows, self.cols, self.recv, self.sent = lead, rows, cols, recv, sent
        row = lax.axis_index("row")
        col = lax.axis_index("col")
        self.y, self.x = row // NX, row % NX
        self.z, self.q = col // 2, col % 2
        self.started = []

    def device(self, dx=0, dy=0, dz=0, dq=0):
        x = (self.x + dx) % NX
        y = (self.y + dy + NY) % NY
        z = (self.z + dz + NZ) % NZ
        q = 1 - self.q if dq else self.q
        return (y * NX + x, z * 2 + q)

    def barrier(self):
        sem = pltpu.get_barrier_semaphore()
        peers = [self.device(dx=d) for d in (1, 2, 3)]
        peers += [self.device(dy=d) for d in (1, -1)]
        peers += [self.device(dz=d) for d in (1, -1)]
        peers += [self.device(dq=1)]
        for peer in peers:
            pl.semaphore_signal(sem, inc=1, device_id=peer, device_id_type=MESH)
        pl.semaphore_wait(sem, len(peers))

    def send(self, cond, slot, device):
        ref, sem = slot
        copy = pltpu.make_async_remote_copy(
            src_ref=ref,
            dst_ref=ref,
            send_sem=self.sent.at[len(self.started)],
            recv_sem=sem,
            device_id=device,
            device_id_type=MESH,
        )

        @pl.when(cond)
        def _():
            copy.start()

        self.started.append((cond, copy))

    def arrive(self, cond, slot):
        ref, sem = slot
        copy = pltpu.make_async_copy(ref, ref, sem)

        @pl.when(cond)
        def _():
            copy.wait()

    def finish(self):
        for cond, copy in self.started:

            @pl.when(cond)
            def _():
                copy.wait_send()

    def lead_slot(self, i, k):
        return self.lead.at[i, k], self.recv.at[i * 4 + k]

    def row_slot(self, k, a):
        return self.rows.at[k, a], self.recv.at[16 + k * 3 + a]

    def col_slot(self, k, b):
        return self.cols.at[k, b], self.recv.at[28 + k * 4 + b]


def spread_tiles(net, cov):
    x, y, z, q = net.x, net.y, net.z, net.q
    always = y >= 0
    top = y == 0
    y_up = y <= 3
    y_down = jnp.logical_or(y == 0, y >= 6)

    @pl.when(top)
    def _():
        for zs in range(2):
            k = q + 2 * zs

            @pl.when(jnp.logical_and(z == zs, x >= k))
            def _():
                ref, sem = net.lead_slot(x, k)
                pltpu.make_async_copy(cov.at[0, 0, 0, 0], ref, sem).start()

        for b in range(4):
            ref, sem = net.col_slot(x, b)
            pltpu.make_async_copy(cov.at[0, 0, b, 0], ref, sem).start()

    for zs in range(2):

        @pl.when(z == zs)
        def _():
            for a in range(3):
                ref, sem = net.row_slot(q + 2 * zs, a)
                pltpu.make_async_copy(cov.at[a, 0, 0, 0], ref, sem).start()

    net.barrier()

    def along_z(cond, zs, slot):
        rel = (z - zs + NZ) % NZ
        net.send(jnp.logical_and(cond, rel <= 5), slot, net.device(dz=1))
        down = jnp.logical_or(rel == 0, rel >= 8)
        net.send(jnp.logical_and(cond, down), slot, net.device(dz=-1))

    def along_y(cond, slot):
        net.send(jnp.logical_and(cond, y_up), slot, net.device(dy=1))
        net.send(jnp.logical_and(cond, y_down), slot, net.device(dy=-1))

    def along_x(cond, slot):
        for dx in (1, 3, 2):
            net.send(cond, slot, net.device(dx=dx))

    def to_partner(cond, slot):
        net.send(cond, slot, net.device(dq=1))

    def rows(zs, a):
        slot = net.row_slot(q + 2 * zs, a)
        net.arrive(always, slot)
        along_z(always, zs, slot)
        to_partner(always, slot)

    def cols(b):
        slot = net.col_slot(x, b)
        net.arrive(always, slot)
        along_y(always, slot)
        along_x(always, slot)

    for zs in range(2):
        k = q + 2 * zs
        slot = net.lead_slot(x, k)
        cond = jnp.logical_and(top, x >= k)
        net.arrive(cond, slot)
        along_z(cond, zs, slot)
        along_y(cond, slot)
        along_x(cond, slot)
        to_partner(cond, slot)
    rows(0, 0)
    rows(1, 0)
    cols(0)
    rows(0, 1)
    rows(1, 1)
    cols(1)
    rows(0, 2)
    rows(1, 2)
    cols(2)
    cols(3)
    for zs in range(2):
        k = q + 2 * zs
        slot = net.lead_slot(x, k)
        cond = jnp.logical_and(y != 0, x >= k)
        net.arrive(cond, slot)
        along_y(cond, slot)
        along_x(cond, slot)
        to_partner(cond, slot)
    for zs in range(2):
        for dx in (1, 3, 2):
            i = (x + dx) % NX
            k = q + 2 * zs
            slot = net.lead_slot(i, k)
            net.arrive(i >= k, slot)
            to_partner(i >= k, slot)
    for zs in range(2):
        for i in range(LEAD_TILES):
            k = 1 - q + 2 * zs
            net.arrive(i >= k, net.lead_slot(i, k))
    for dx in (1, 3, 2):
        for b in range(4):
            net.arrive(always, net.col_slot((x + dx) % NX, b))
    for zs in range(2):
        for a in range(3):
            net.arrive(always, net.row_slot(1 - q + 2 * zs, a))
    net.finish()


def factor_tile(work):
    sub = lax.broadcasted_iota(jnp.int32, (8, 128), 0)

    def across(value, k):
        return jnp.broadcast_to(value[k : k + 1, :], (8, 128))

    def along(value, k):
        return jnp.broadcast_to(value[:, k : k + 1], (8, 128))

    for block in range(16):
        r0 = 8 * block
        last = block == 15
        xa = work[r0 : r0 + 8, 0:128]
        xe = work[r0 : r0 + 8, 128:256]
        here = [along(xa, r0 + k) for k in range(8)]
        if not last:
            na = work[r0 + 8 : r0 + 16, 0:128]
            ne = work[r0 + 8 : r0 + 16, 128:256]
            below = [along(na, r0 + k) for k in range(8)]
        pivots = jnp.ones((8, 128), f32)
        for k in range(8):
            pivot = across(here[k], k)
            inverse = 1.0 / pivot
            ra = across(xa, k)
            re = across(xe, k)
            m = jnp.where(sub > k, here[k] * inverse, 0.0)
            pivots = jnp.where(sub == k, pivot, pivots)
            if not last:
                n = below[k] * inverse
            for j in range(k + 1, 8):
                entry = across(here[j], k)
                here[j] = here[j] - m * entry
                if not last:
                    below[j] = below[j] - n * entry
            xa = xa - m * ra
            xe = xe - m * re
            if not last:
                na = na - n * ra
                ne = ne - n * re
        scale = lax.rsqrt(pivots)
        ua = xa * scale
        ue = xe * scale
        work[r0 : r0 + 8, 0:128] = ua
        work[r0 : r0 + 8, 128:256] = ue
        if not last:
            work[r0 + 8 : r0 + 16, 0:128] = na
            work[r0 + 8 : r0 + 16, 128:256] = ne
        if block < 14:
            q0 = r0 + 16
            update = dot(ua, jnp.concatenate([ua, ue], axis=1), TN)
            work[q0:, :] = work[q0:, :] - update[q0:, :]


def kernel(mask, cov, out, lead, rows, cols, own, work, left, right, recv, sent, own_sem):
    r = lax.axis_index("row")
    c = lax.axis_index("col")
    own_copy = pltpu.make_async_copy(cov.at[:, 0, :, 0], own, own_sem)
    own_copy.start()
    spread_tiles(Spread(lead, rows, cols, recv, sent), cov)
    across = lax.broadcasted_iota(jnp.int32, (128, 128), 1)
    down = lax.broadcasted_iota(jnp.int32, (128, 128), 0)
    eye = (across == down).astype(f32)
    for k in range(LEAD_TILES):
        here = slice(128 * k, 128 * k + 128)
        work[:, 0:128] = lead[k, k]
        work[:, 128:256] = eye
        factor_tile(work)
        inverse = work[:, 128:256]
        for i in range(k + 1, LEAD_TILES):
            lead[i, k] = dot(lead[i, k], inverse, NT)
        for i in range(k + 1, LEAD_TILES):
            for j in range(k + 1, i + 1):
                lead[i, j] = lead[i, j] - dot(lead[i, k], lead[j, k], NT)
        raw = jnp.concatenate(
            [cols[k, b] * mask[k, b * 24 + c].astype(f32) for b in range(4)], axis=1
        )
        for j in range(k):
            raw = raw - dot(lead[k, j], right[128 * j : 128 * j + 128, :])
        right[here, :] = dot(inverse, raw)
        for a in range(3):
            raw = rows[k, a] * mask[a * 32 + r, k].astype(f32)
            for j in range(k):
                raw = raw - dot(left[a, :, 128 * j : 128 * j + 128], lead[k, j], NT)
            left[a, :, here] = dot(raw, inverse, NT)
    own_copy.wait()
    pick = pl.ds(pl.multiple_of(jnp.minimum(c, 3) * 128, 128), 128)
    for a in range(3):
        tile_row = a * 32 + r
        product = dot(left[a], right[...])
        for b in range(4):
            masked = own[a, b] * mask[tile_row, b * 24 + c].astype(f32)
            value = masked - product[:, 128 * b : 128 * b + 128]
            if a == 0:
                value = jnp.where(r < LEAD_TILES, 0.0, value)
            if b == 0:
                lower = (tile_row - c) * 128 + down >= across
                value = jnp.where(c < LEAD_TILES, jnp.where(lower, left[a, :, pick], 0.0), value)
            out[a, 0, b, 0] = value.astype(jnp.bfloat16)


def on_device(covariance, tile_mask):
    vmem = pltpu.VMEM
    return pl.pallas_call(
        kernel,
        out_shape=jax.ShapeDtypeStruct(covariance.shape, jnp.bfloat16),
        in_specs=[pl.BlockSpec(memory_space=pltpu.SMEM), pl.BlockSpec(memory_space=pl.ANY)],
        out_specs=pl.BlockSpec(memory_space=vmem),
        scratch_shapes=[
            vmem((4, 4, 128, 128), f32),
            vmem((4, 3, 128, 128), f32),
            vmem((4, 4, 128, 128), f32),
            vmem((3, 4, 128, 128), f32),
            vmem((128, 256), f32),
            vmem((3, 128, 512), f32),
            vmem((512, 512), f32),
            pltpu.SemaphoreType.DMA((44,)),
            pltpu.SemaphoreType.DMA((SEND_SEMS,)),
            pltpu.SemaphoreType.DMA,
        ],
        compiler_params=pltpu.CompilerParams(collective_id=0, has_side_effects=True),
        name="panels",
    )(tile_mask, covariance)


def solution(mesh):
    in_specs = (P(None, "row", None, "col", None, None), P())
    out_specs = P(None, "row", None, "col", None, None)
    return jax.shard_map(
        on_device, mesh=mesh, in_specs=in_specs, out_specs=out_specs, check_vma=False
    )
```

```python
import functools

import jax
import jax.numpy as jnp
from jax import lax
from jax.experimental import pallas as pl
from jax.experimental.pallas import tpu as pltpu
from jax.sharding import PartitionSpec as P

MESH = pl.DeviceIdType.MESH
f32 = jnp.float32
NN = (((1,), (0,)), ((), ()))
NT = (((1,), (1,)), ((), ()))
TN = (((0,), (0,)), ((), ()))
NX = 4
NY = 8
NZ = 12
LEAD_TILES = 4
PIECE = 16


def dot(a, b, dims=NN):
    return lax.dot_general(
        a, b, dims, precision=lax.Precision.HIGHEST, preferred_element_type=f32
    )


def factor_tile(work):
    sub = lax.broadcasted_iota(jnp.int32, (8, 128), 0)

    def across(value, k):
        return jnp.broadcast_to(value[k : k + 1, :], (8, 128))

    def along(value, k):
        return jnp.broadcast_to(value[:, k : k + 1], (8, 128))

    for block in range(16):
        r0 = 8 * block
        last = block == 15
        xa = work[r0 : r0 + 8, 0:128]
        xe = work[r0 : r0 + 8, 128:256]
        here = [along(xa, r0 + k) for k in range(8)]
        if not last:
            na = work[r0 + 8 : r0 + 16, 0:128]
            ne = work[r0 + 8 : r0 + 16, 128:256]
            below = [along(na, r0 + k) for k in range(8)]
        pivots = jnp.ones((8, 128), f32)
        for k in range(8):
            pivot = across(here[k], k)
            inverse = 1.0 / pivot
            ra = across(xa, k)
            re = across(xe, k)
            m = jnp.where(sub > k, here[k] * inverse, 0.0)
            pivots = jnp.where(sub == k, pivot, pivots)
            if not last:
                n = below[k] * inverse
            for j in range(k + 1, 8):
                entry = across(here[j], k)
                here[j] = here[j] - m * entry
                if not last:
                    below[j] = below[j] - n * entry
            xa = xa - m * ra
            xe = xe - m * re
            if not last:
                na = na - n * ra
                ne = ne - n * re
        scale = lax.rsqrt(pivots)
        ua = xa * scale
        ue = xe * scale
        work[r0 : r0 + 8, 0:128] = ua
        work[r0 : r0 + 8, 128:256] = ue
        if not last:
            work[r0 + 8 : r0 + 16, 0:128] = na
            work[r0 + 8 : r0 + 16, 128:256] = ne
        if block < 14:
            q0 = r0 + 16
            update = dot(ua, jnp.concatenate([ua, ue], axis=1), TN)
            work[q0:, :] = work[q0:, :] - update[q0:, :]


class Net:
    def __init__(self, recv, sent):
        self.recv, self.sent = recv, sent
        row = lax.axis_index("row")
        col = lax.axis_index("col")
        self.y, self.x = row // NX, row % NX
        self.z, self.q = col // 2, col % 2
        self.started = []
        self.slots = {}
        self.arrivals = {}

    def device(self, dx=0, dy=0, dz=0, dq=0):
        x = (self.x + dx) % NX
        y = (self.y + dy + NY) % NY
        z = (self.z + dz + NZ) % NZ
        q = (self.q + dq) % 2
        return (y * NX + x, z * 2 + q)

    def group(self):
        return [
            self.device(dx=dx, dq=dq) for dx in (2, 1, 3, 0) for dq in (0, 1) if dx or dq
        ]

    def column(self):
        return [self.device(dy=dy) for dy in (4, 3, -3, 2, -2, 1, -1)]

    def ring(self):
        return [self.device(dz=dz) for dz in (6, 5, -5, 4, -4, 3, -3, 2, -2, 1, -1)]

    def barrier(self):
        sem = pltpu.get_barrier_semaphore()
        peers = self.ring() + self.column() + self.group()
        for peer in peers:
            pl.semaphore_signal(sem, inc=1, device_id=peer, device_id_type=MESH)
        pl.semaphore_wait(sem, len(peers))

    def send(self, cond, key, slot, device):
        ref, sem = slot
        index = self.slots.setdefault(key, len(self.slots))
        copy = pltpu.make_async_remote_copy(
            src_ref=ref,
            dst_ref=ref,
            send_sem=self.sent.at[index],
            recv_sem=self.recv.at[sem],
            device_id=device,
            device_id_type=MESH,
        )

        @pl.when(cond)
        def _():
            copy.start()

        self.started.append((cond, copy))

    def load(self, cond, source, slot):
        ref, sem = slot

        @pl.when(cond)
        def _():
            pltpu.make_async_copy(source, ref, self.recv.at[sem]).start()

    def arrive(self, cond, slot):
        ref, sem = slot

        @pl.when(cond)
        def _():
            pltpu.make_async_copy(ref, ref, self.recv.at[sem]).wait()

    def finish(self):
        for cond, copy in self.started:

            @pl.when(cond)
            def _():
                copy.wait_send()


RAW_SEM, ROW_SEM, COL_SEM, PIECE_SEM = 0, 16, 28, 44
RECV_SEMS = 76
SEND_SEMS = 125


def kernel(
    mask, cov, out, raw, trail, factor, rows, cols, own, work, left, right, schur, recv, sent,
    own_sem,
):
    r = lax.axis_index("row")
    c = lax.axis_index("col")
    net = Net(recv, sent)
    x, y, z, q = net.x, net.y, net.z, net.q
    both = jnp.logical_and
    always = y >= 0
    top = y == 0
    factors = both(top, z == 0)
    relays = jnp.logical_not(factors)
    own_copy = pltpu.make_async_copy(cov.at[:, 0, :, 0], own, own_sem)
    piece_of = x * 2 + q

    def raw_slot(i, k):
        return raw.at[i, k], RAW_SEM + i * 4 + k

    def row_slot(k, a):
        return rows.at[k, a], ROW_SEM + k * 3 + a

    def col_slot(k, b):
        return cols.at[k, b], COL_SEM + k * 4 + b

    def piece_slot(k, piece):
        span = pl.ds(pl.multiple_of(piece * PIECE, PIECE), PIECE)
        return factor.at[k, pl.ds(0, 4 - k), span], PIECE_SEM + k * 8 + piece

    near = both(factors, x >= q)
    far = both(both(top, z == 1), x >= q + 2)
    net.load(near, cov.at[0, 0, 0, 0], raw_slot(x, q))
    net.load(far, cov.at[0, 0, 0, 0], raw_slot(x, q + 2))
    for b in range(4):
        net.load(top, cov.at[0, 0, b, 0], col_slot(x, b))
    for zs in range(2):
        for a in range(3):
            net.load(z == zs, cov.at[a, 0, 0, 0], row_slot(q + 2 * zs, a))
    own_copy.start()
    net.barrier()

    def send_raw(cond, k, tag):
        slot = raw_slot(x, k)
        net.arrive(cond, slot)
        for n, peer in enumerate(net.group()):
            net.send(cond, ("raw", tag, n), slot, peer)

    def send_rows(cond, zs, a):
        slot = row_slot(q + 2 * zs, a)
        net.arrive(cond, slot)
        rel = (z - zs + NZ) % NZ
        up = rel <= 5
        down = jnp.logical_or(rel == 0, rel >= 8)
        net.send(both(cond, up), ("row", zs, a, 0), slot, net.device(dz=1))
        net.send(both(cond, down), ("row", zs, a, 1), slot, net.device(dz=-1))
        net.send(cond, ("row", zs, a, 2), slot, net.device(dq=1))

    def send_cols(cond, b):
        slot = col_slot(x, b)
        net.arrive(cond, slot)
        up = y <= 3
        down = jnp.logical_or(y == 0, y >= 6)
        net.send(both(cond, up), ("col", b, 0), slot, net.device(dy=1))
        net.send(both(cond, down), ("col", b, 1), slot, net.device(dy=-1))
        for dx in range(1, NX):
            net.send(cond, ("col", b, 1 + dx), slot, net.device(dx=dx))

    send_raw(near, q, 0)
    net.arrive(far, raw_slot(x, q + 2))
    net.send(far, ("raw", 1, 7), raw_slot(x, q + 2), net.device(dz=-1))
    passed = both(factors, x >= q + 2)
    send_raw(passed, q + 2, 1)
    for a in range(3):
        for zs in range(2):
            send_rows(z == zs, zs, a)
    for b in range(4):
        send_cols(top, b)

    across = lax.broadcasted_iota(jnp.int32, (128, 128), 1)
    down = lax.broadcasted_iota(jnp.int32, (128, 128), 0)

    def raw_arrive(i, k):
        net.arrive(both(factors, both(jnp.logical_or(x != i, q != k % 2), True)), raw_slot(i, k))

    for k in range(LEAD_TILES):
        if k == 0:
            raw_arrive(0, 0)

        @pl.when(factors)
        def _():
            work[:, 0:128] = raw[0, 0] if k == 0 else trail[k, k]
            work[:, 128:256] = (across == down).astype(f32)
            factor_tile(work)
            factor[k, 0] = work[:, 128:256]

        if k == 0:
            for i in range(1, LEAD_TILES):
                raw_arrive(i, 0)

        @pl.when(factors)
        def _():
            for i in range(k + 1, LEAD_TILES):
                tile = raw[i, 0] if k == 0 else trail[i, k]
                factor[k, i - k] = dot(tile, work[:, 128:256], NT)

        slot = piece_slot(k, piece_of)
        for n, peer in enumerate(net.ring() + net.column()):
            net.send(factors, ("piece", k, n), slot, peer)
        if k == 0:
            for i in range(1, LEAD_TILES):
                for j in range(1, i + 1):
                    raw_arrive(i, j)

        @pl.when(factors)
        def _():
            for i in range(k + 1, LEAD_TILES):
                for j in range(k + 1, i + 1):
                    old = raw[i, j] if k == 0 else trail[i, j]
                    trail[i, j] = old - dot(factor[k, i - k], factor[k, j - k], NT)

        if k == 0:
            for a in range(3):
                send_rows(factors, 1, a)

    for a in range(3):
        for zs in range(2):
            send_rows(both(relays, z != zs), zs, a)
        send_cols(jnp.logical_not(top), a)
    send_cols(jnp.logical_not(top), 3)
    for dx in range(1, NX):
        for b in range(4):
            net.arrive(always, col_slot((x + dx) % NX, b))
    for zs in range(2):
        for a in range(3):
            net.arrive(always, row_slot(1 - q + 2 * zs, a))
    for k in range(LEAD_TILES):
        for b in range(4):
            right[k, :, 128 * b : 128 * b + 128] = cols[k, b] * mask[k, b * 24 + c].astype(f32)
        for a in range(3):
            left[k, 128 * a : 128 * a + 128, :] = rows[k, a] * mask[a * 32 + r, k].astype(f32)
    own_copy.wait()
    for a in range(3):
        for b in range(4):
            schur[128 * a : 128 * a + 128, 128 * b : 128 * b + 128] = own[a, b] * mask[
                a * 32 + r, b * 24 + c
            ].astype(f32)

    passing = both(relays, top)
    for k in range(LEAD_TILES):
        slot = piece_slot(k, piece_of)
        net.arrive(relays, slot)
        for n, peer in enumerate(net.column()):
            net.send(passing, ("piece", k, 11 + n), slot, peer)
        for n, peer in enumerate(net.group()):
            net.send(relays, ("piece", k, n), slot, peer)
        for n in range(1, 8):
            net.arrive(relays, piece_slot(k, (piece_of + n) % 8))
        inverse = factor[k, 0]
        zk = dot(inverse, right[k])
        yk = dot(left[k], inverse, NT)
        left[k] = yk
        for i in range(k + 1, LEAD_TILES):
            lower = factor[k, i - k]
            right[i] = right[i] - dot(lower, zk)
            left[i] = left[i] - dot(yk, lower, NT)
        schur[...] = schur[...] - dot(yk, zk)

    edge = jnp.minimum(c, 3)
    for a in range(3):
        tile_row = a * 32 + r
        for b in range(4):
            value = schur[128 * a : 128 * a + 128, 128 * b : 128 * b + 128]
            if a == 0:
                value = jnp.where(r < LEAD_TILES, 0.0, value)
            if b == 0:
                lower = (tile_row - c) * 128 + down >= across
                column = jnp.where(lower, left[edge, 128 * a : 128 * a + 128, :], 0.0)
                value = jnp.where(c < LEAD_TILES, column, value)
            out[a, 0, b, 0] = value.astype(jnp.bfloat16)
    net.finish()


def on_device(covariance, tile_mask):
    vmem = pltpu.VMEM
    return pl.pallas_call(
        kernel,
        out_shape=jax.ShapeDtypeStruct(covariance.shape, jnp.bfloat16),
        in_specs=[pl.BlockSpec(memory_space=pltpu.SMEM), pl.BlockSpec(memory_space=pl.ANY)],
        out_specs=pl.BlockSpec(memory_space=vmem),
        scratch_shapes=[
            vmem((4, 4, 128, 128), f32),
            vmem((4, 4, 128, 128), f32),
            vmem((4, 4, 128, 128), f32),
            vmem((4, 3, 128, 128), f32),
            vmem((4, 4, 128, 128), f32),
            vmem((3, 4, 128, 128), f32),
            vmem((128, 256), f32),
            vmem((4, 384, 128), f32),
            vmem((4, 128, 512), f32),
            vmem((384, 512), f32),
            pltpu.SemaphoreType.DMA((RECV_SEMS,)),
            pltpu.SemaphoreType.DMA((SEND_SEMS,)),
            pltpu.SemaphoreType.DMA,
        ],
        compiler_params=pltpu.CompilerParams(collective_id=0, has_side_effects=True),
        name="panels",
    )(tile_mask, covariance)


def solution(mesh):
    in_specs = (P(None, "row", None, "col", None, None), P())
    out_specs = P(None, "row", None, "col", None, None)
    return jax.shard_map(
        on_device, mesh=mesh, in_specs=in_specs, out_specs=out_specs, check_vma=False
    )
```

```python
import functools

import jax
import jax.numpy as jnp
from jax import lax
from jax.experimental import pallas as pl
from jax.experimental.pallas import tpu as pltpu
from jax.sharding import PartitionSpec as P

MESH = pl.DeviceIdType.MESH
f32 = jnp.float32
NN = (((1,), (0,)), ((), ()))
NT = (((1,), (1,)), ((), ()))
TN = (((0,), (0,)), ((), ()))
NX = 4
NY = 8
NZ = 12
LEAD_TILES = 4
PIECE = 16


def dot(a, b, dims=NN):
    return lax.dot_general(
        a, b, dims, precision=lax.Precision.HIGHEST, preferred_element_type=f32
    )


def factor_tile(work):
    sub = lax.broadcasted_iota(jnp.int32, (8, 128), 0)

    def across(value, k):
        return jnp.broadcast_to(value[k : k + 1, :], (8, 128))

    def along(value, k):
        return jnp.broadcast_to(value[:, k : k + 1], (8, 128))

    for group in range(4):
        q0 = 32 * group
        xa = [work[q0 + 8 * i : q0 + 8 * i + 8, 0:128] for i in range(4)]
        xe = [work[q0 + 8 * i : q0 + 8 * i + 8, 128:256] for i in range(4)]
        for block in range(4):
            live = range(block, 4)
            heads = {i: [along(xa[i], q0 + 8 * block + k) for k in range(8)] for i in live}
            pivots = jnp.ones((8, 128), f32)
            for k in range(8):
                pivot = across(heads[block][k], k)
                inverse = 1.0 / pivot
                ra = across(xa[block], k)
                re = across(xe[block], k)
                pivots = jnp.where(sub == k, pivot, pivots)
                m = {i: heads[i][k] * inverse for i in live}
                m[block] = jnp.where(sub > k, m[block], 0.0)
                for j in range(k + 1, 8):
                    entry = across(heads[block][j], k)
                    for i in live:
                        heads[i][j] = heads[i][j] - m[i] * entry
                for i in live:
                    xa[i] = xa[i] - m[i] * ra
                    xe[i] = xe[i] - m[i] * re
            scale = lax.rsqrt(pivots)
            xa[block] = xa[block] * scale
            xe[block] = xe[block] * scale
            r0 = q0 + 8 * block
            work[r0 : r0 + 8, 0:128] = xa[block]
            work[r0 : r0 + 8, 128:256] = xe[block]
        if group < 3:
            upper = jnp.concatenate(xa, axis=0)
            both = jnp.concatenate([upper, jnp.concatenate(xe, axis=0)], axis=1)
            turned = upper.T
            q1, q2 = q0 + 32, q0 + 64
            work[q1:q2, :] = work[q1:q2, :] - dot(turned[q1:q2, :], both)
            if group < 2:
                work[q2:, :] = work[q2:, :] - dot(turned[q2:, :], both)


class Net:
    def __init__(self, recv, sent):
        self.recv, self.sent = recv, sent
        row = lax.axis_index("row")
        col = lax.axis_index("col")
        self.y, self.x = row // NX, row % NX
        self.z, self.q = col // 2, col % 2
        self.started = []
        self.slots = {}
        self.arrivals = {}

    def device(self, dx=0, dy=0, dz=0, dq=0):
        x = (self.x + dx) % NX
        y = (self.y + dy + NY) % NY
        z = (self.z + dz + NZ) % NZ
        q = (self.q + dq) % 2
        return (y * NX + x, z * 2 + q)

    def group(self):
        return [
            self.device(dx=dx, dq=dq) for dx in (2, 1, 3, 0) for dq in (0, 1) if dx or dq
        ]

    def column(self):
        return [self.device(dy=dy) for dy in (4, 3, -3, 2, -2, 1, -1)]

    def ring(self):
        return [self.device(dz=dz) for dz in (6, 5, -5, 4, -4, 3, -3, 2, -2, 1, -1)]

    def barrier(self):
        sem = pltpu.get_barrier_semaphore()
        peers = self.ring() + self.column() + self.group()
        for peer in peers:
            pl.semaphore_signal(sem, inc=1, device_id=peer, device_id_type=MESH)
        pl.semaphore_wait(sem, len(peers))

    def send(self, cond, key, slot, device):
        ref, sem = slot
        index = self.slots.setdefault(key, len(self.slots))
        copy = pltpu.make_async_remote_copy(
            src_ref=ref,
            dst_ref=ref,
            send_sem=self.sent.at[index],
            recv_sem=self.recv.at[sem],
            device_id=device,
            device_id_type=MESH,
        )

        @pl.when(cond)
        def _():
            copy.start()

        self.started.append((cond, copy))

    def load(self, cond, source, slot):
        ref, sem = slot

        @pl.when(cond)
        def _():
            pltpu.make_async_copy(source, ref, self.recv.at[sem]).start()

    def arrive(self, cond, slot):
        ref, sem = slot

        @pl.when(cond)
        def _():
            pltpu.make_async_copy(ref, ref, self.recv.at[sem]).wait()

    def finish(self):
        for cond, copy in self.started:

            @pl.when(cond)
            def _():
                copy.wait_send()


RAW_SEM, ROW_SEM, COL_SEM, PIECE_SEM = 0, 16, 28, 44
RECV_SEMS = 76
SEND_SEMS = 125


def kernel(
    mask, cov, out, raw, trail, factor, rows, cols, own, work, left, right, schur, recv, sent,
    own_sem,
):
    r = lax.axis_index("row")
    c = lax.axis_index("col")
    net = Net(recv, sent)
    x, y, z, q = net.x, net.y, net.z, net.q
    both = jnp.logical_and
    always = y >= 0
    top = y == 0
    factors = both(top, z == 0)
    relays = jnp.logical_not(factors)
    own_copy = pltpu.make_async_copy(cov.at[:, 0, :, 0], own, own_sem)
    piece_of = x * 2 + q

    def raw_slot(i, k):
        return raw.at[i, k], RAW_SEM + i * 4 + k

    def row_slot(k, a):
        return rows.at[k, a], ROW_SEM + k * 3 + a

    def col_slot(k, b):
        return cols.at[k, b], COL_SEM + k * 4 + b

    def piece_slot(k, piece):
        span = pl.ds(pl.multiple_of(piece * PIECE, PIECE), PIECE)
        return factor.at[k, pl.ds(0, 4 - k), span], PIECE_SEM + k * 8 + piece

    near = both(factors, x >= q)
    far = both(both(top, z == 1), x >= q + 2)
    net.load(near, cov.at[0, 0, 0, 0], raw_slot(x, q))
    net.load(far, cov.at[0, 0, 0, 0], raw_slot(x, q + 2))
    for b in range(4):
        net.load(top, cov.at[0, 0, b, 0], col_slot(x, b))
    for zs in range(2):
        for a in range(3):
            net.load(z == zs, cov.at[a, 0, 0, 0], row_slot(q + 2 * zs, a))
    own_copy.start()
    net.barrier()

    def send_raw(cond, k, tag):
        slot = raw_slot(x, k)
        net.arrive(cond, slot)
        for n, peer in enumerate(net.group()):
            net.send(cond, ("raw", tag, n), slot, peer)

    def send_rows(cond, zs, a):
        slot = row_slot(q + 2 * zs, a)
        net.arrive(cond, slot)
        rel = (z - zs + NZ) % NZ
        up = rel <= 5
        down = jnp.logical_or(rel == 0, rel >= 8)
        net.send(both(cond, up), ("row", zs, a, 0), slot, net.device(dz=1))
        net.send(both(cond, down), ("row", zs, a, 1), slot, net.device(dz=-1))
        net.send(cond, ("row", zs, a, 2), slot, net.device(dq=1))

    def cols_along_y(cond, b):
        slot = col_slot(x, b)
        net.arrive(cond, slot)
        up = y <= 3
        down = jnp.logical_or(y == 0, y >= 6)
        net.send(both(cond, up), ("col", b, 0), slot, net.device(dy=1))
        net.send(both(cond, down), ("col", b, 1), slot, net.device(dy=-1))

    def cols_along_x(cond, b):
        slot = col_slot(x, b)
        for dx in range(1, NX):
            net.send(cond, ("col", b, 1 + dx), slot, net.device(dx=dx))

    send_raw(near, q, 0)
    net.arrive(far, raw_slot(x, q + 2))
    net.send(far, ("raw", 1, 7), raw_slot(x, q + 2), net.device(dz=-1))
    for a in range(3):
        for zs in range(2):
            send_rows(z == zs, zs, a)
        cols_along_y(top, a)
        cols_along_x(both(top, relays), a)
    cols_along_y(top, 3)
    cols_along_x(both(top, relays), 3)
    passed = both(factors, x >= q + 2)
    send_raw(passed, q + 2, 1)

    across = lax.broadcasted_iota(jnp.int32, (128, 128), 1)
    down = lax.broadcasted_iota(jnp.int32, (128, 128), 0)

    def raw_arrive(i, k):
        net.arrive(both(factors, both(jnp.logical_or(x != i, q != k % 2), True)), raw_slot(i, k))

    for k in range(LEAD_TILES):
        if k == 0:
            raw_arrive(0, 0)
            for b in range(4):
                cols_along_x(factors, b)

        @pl.when(factors)
        def _():
            work[:, 0:128] = raw[0, 0] if k == 0 else trail[k, k]
            work[:, 128:256] = (across == down).astype(f32)
            factor_tile(work)
            factor[k, 0] = work[:, 128:256]

        if k == 0:
            for i in range(1, LEAD_TILES):
                raw_arrive(i, 0)

        @pl.when(factors)
        def _():
            for i in range(k + 1, LEAD_TILES):
                tile = raw[i, 0] if k == 0 else trail[i, k]
                factor[k, i - k] = dot(tile, work[:, 128:256], NT)

        slot = piece_slot(k, piece_of)
        for n, peer in enumerate(net.ring() + net.column()):
            net.send(factors, ("piece", k, n), slot, peer)
        if k == 0:
            for i in range(1, LEAD_TILES):
                for j in range(1, i + 1):
                    raw_arrive(i, j)

        @pl.when(factors)
        def _():
            for i in range(k + 1, LEAD_TILES):
                for j in range(k + 1, i + 1):
                    old = raw[i, j] if k == 0 else trail[i, j]
                    trail[i, j] = old - dot(factor[k, i - k], factor[k, j - k], NT)

        if k == 0:
            for a in range(3):
                send_rows(factors, 1, a)

    passing = both(relays, top)
    below = jnp.logical_not(top)

    def pass_piece(k):
        slot = piece_slot(k, piece_of)
        net.arrive(relays, slot)
        for n, peer in enumerate(net.column()):
            net.send(passing, ("piece", k, 11 + n), slot, peer)
        for n, peer in enumerate(net.group()):
            net.send(relays, ("piece", k, n), slot, peer)

    def take_pieces(k):
        for n in range(1, 8):
            net.arrive(relays, piece_slot(k, (piece_of + n) % 8))

    def apply_column(k):
        inverse = factor[k, 0]
        zk = dot(inverse, right[k])
        yk = dot(left[k], inverse, NT)
        left[k] = yk
        for i in range(k + 1, LEAD_TILES):
            lower = factor[k, i - k]
            right[i] = right[i] - dot(lower, zk)
            left[i] = left[i] - dot(yk, lower, NT)
        schur[...] = schur[...] - dot(yk, zk)

    for b in range(4):
        if b < 3:
            for zs in range(2):
                send_rows(both(relays, z != zs), zs, b)
        cols_along_y(below, b)
        cols_along_x(below, b)
    pass_piece(0)
    own_copy.wait()
    for a in range(3):
        for b in range(4):
            schur[128 * a : 128 * a + 128, 128 * b : 128 * b + 128] = own[a, b] * mask[
                a * 32 + r, b * 24 + c
            ].astype(f32)
    for dx in range(1, NX):
        for b in range(4):
            net.arrive(always, col_slot((x + dx) % NX, b))
    for k in range(LEAD_TILES):
        for b in range(4):
            right[k, :, 128 * b : 128 * b + 128] = cols[k, b] * mask[k, b * 24 + c].astype(f32)
    pass_piece(1)
    for zs in range(2):
        for a in range(3):
            net.arrive(always, row_slot(1 - q + 2 * zs, a))
    for k in range(LEAD_TILES):
        for a in range(3):
            left[k, 128 * a : 128 * a + 128, :] = rows[k, a] * mask[a * 32 + r, k].astype(f32)
    take_pieces(0)
    apply_column(0)
    pass_piece(2)
    take_pieces(1)
    apply_column(1)
    pass_piece(3)
    take_pieces(2)
    apply_column(2)
    take_pieces(3)
    apply_column(3)

    edge = jnp.minimum(c, 3)
    for a in range(3):
        tile_row = a * 32 + r
        for b in range(4):
            value = schur[128 * a : 128 * a + 128, 128 * b : 128 * b + 128]
            if a == 0:
                value = jnp.where(r < LEAD_TILES, 0.0, value)
            if b == 0:
                lower = (tile_row - c) * 128 + down >= across
                column = jnp.where(lower, left[edge, 128 * a : 128 * a + 128, :], 0.0)
                value = jnp.where(c < LEAD_TILES, column, value)
            out[a, 0, b, 0] = value.astype(jnp.bfloat16)
    net.finish()


def on_device(covariance, tile_mask):
    vmem = pltpu.VMEM
    return pl.pallas_call(
        kernel,
        out_shape=jax.ShapeDtypeStruct(covariance.shape, jnp.bfloat16),
        in_specs=[pl.BlockSpec(memory_space=pltpu.SMEM), pl.BlockSpec(memory_space=pl.ANY)],
        out_specs=pl.BlockSpec(memory_space=vmem),
        scratch_shapes=[
            vmem((4, 4, 128, 128), f32),
            vmem((4, 4, 128, 128), f32),
            vmem((4, 4, 128, 128), f32),
            vmem((4, 3, 128, 128), f32),
            vmem((4, 4, 128, 128), f32),
            vmem((3, 4, 128, 128), f32),
            vmem((128, 256), f32),
            vmem((4, 384, 128), f32),
            vmem((4, 128, 512), f32),
            vmem((384, 512), f32),
            pltpu.SemaphoreType.DMA((RECV_SEMS,)),
            pltpu.SemaphoreType.DMA((SEND_SEMS,)),
            pltpu.SemaphoreType.DMA,
        ],
        compiler_params=pltpu.CompilerParams(collective_id=0, has_side_effects=True),
        name="panels",
    )(tile_mask, covariance)


def solution(mesh):
    in_specs = (P(None, "row", None, "col", None, None), P())
    out_specs = P(None, "row", None, "col", None, None)
    return jax.shard_map(
        on_device, mesh=mesh, in_specs=in_specs, out_specs=out_specs, check_vma=False
    )
```

```python
import functools

import jax
import jax.numpy as jnp
from jax import lax
from jax.experimental import pallas as pl
from jax.experimental.pallas import tpu as pltpu
from jax.sharding import PartitionSpec as P

MESH = pl.DeviceIdType.MESH
f32 = jnp.float32
NN = (((1,), (0,)), ((), ()))
NT = (((1,), (1,)), ((), ()))
TN = (((0,), (0,)), ((), ()))
NX = 4
NY = 8
NZ = 12
LEAD_TILES = 4
PIECE = 16


def dot(a, b, dims=NN):
    return lax.dot_general(
        a, b, dims, precision=lax.Precision.HIGHEST, preferred_element_type=f32
    )


def factor_tile(work):
    sub = lax.broadcasted_iota(jnp.int32, (8, 128), 0)

    def across(value, k):
        return jnp.broadcast_to(value[k : k + 1, :], (8, 128))

    def along(value, k):
        return jnp.broadcast_to(value[:, k : k + 1], (8, 128))

    for group in range(4):
        q0 = 32 * group
        xa = [work[q0 + 8 * i : q0 + 8 * i + 8, 0:128] for i in range(4)]
        xe = [work[q0 + 8 * i : q0 + 8 * i + 8, 128:256] for i in range(4)]
        for block in range(4):
            live = range(block, 4)
            heads = {i: [along(xa[i], q0 + 8 * block + k) for k in range(8)] for i in live}
            pivots = jnp.ones((8, 128), f32)
            for k in range(8):
                pivot = across(heads[block][k], k)
                inverse = 1.0 / pivot
                ra = across(xa[block], k)
                re = across(xe[block], k)
                pivots = jnp.where(sub == k, pivot, pivots)
                m = {i: heads[i][k] * inverse for i in live}
                m[block] = jnp.where(sub > k, m[block], 0.0)
                for j in range(k + 1, 8):
                    entry = across(heads[block][j], k)
                    for i in live:
                        heads[i][j] = heads[i][j] - m[i] * entry
                for i in live:
                    xa[i] = xa[i] - m[i] * ra
                    xe[i] = xe[i] - m[i] * re
            scale = lax.rsqrt(pivots)
            xa[block] = xa[block] * scale
            xe[block] = xe[block] * scale
            r0 = q0 + 8 * block
            work[r0 : r0 + 8, 0:128] = xa[block]
            work[r0 : r0 + 8, 128:256] = xe[block]
        if group < 3:
            upper = jnp.concatenate(xa, axis=0)
            both = jnp.concatenate([upper, jnp.concatenate(xe, axis=0)], axis=1)
            turned = upper.T
            q1, q2 = q0 + 32, q0 + 64
            work[q1:q2, :] = work[q1:q2, :] - dot(turned[q1:q2, :], both)
            if group < 2:
                work[q2:, :] = work[q2:, :] - dot(turned[q2:, :], both)


def split(value):
    high = value.astype(jnp.bfloat16)
    return high, (value - high.astype(f32)).astype(jnp.bfloat16)


def split_dot(a, b, dims=NN):
    def part(i, j):
        return lax.dot_general(a[i], b[j], dims, preferred_element_type=f32)

    return part(0, 0) + (part(0, 1) + part(1, 0))


class Net:
    def __init__(self, recv, sent):
        self.recv, self.sent = recv, sent
        row = lax.axis_index("row")
        col = lax.axis_index("col")
        self.y, self.x = row // NX, row % NX
        self.z, self.q = col // 2, col % 2
        self.started = []
        self.slots = {}
        self.arrivals = {}

    def device(self, dx=0, dy=0, dz=0, dq=0):
        x = (self.x + dx) % NX
        y = (self.y + dy + NY) % NY
        z = (self.z + dz + NZ) % NZ
        q = (self.q + dq) % 2
        return (y * NX + x, z * 2 + q)

    def group(self):
        return [
            self.device(dx=dx, dq=dq) for dx in (2, 1, 3, 0) for dq in (0, 1) if dx or dq
        ]

    def column(self):
        return [self.device(dy=dy) for dy in (4, 3, -3, 2, -2, 1, -1)]

    def ring(self):
        return [self.device(dz=dz) for dz in (6, 5, -5, 4, -4, 3, -3, 2, -2, 1, -1)]

    def barrier(self):
        sem = pltpu.get_barrier_semaphore()
        peers = self.ring() + self.column() + self.group()
        for peer in peers:
            pl.semaphore_signal(sem, inc=1, device_id=peer, device_id_type=MESH)
        pl.semaphore_wait(sem, len(peers))

    def send(self, cond, key, slot, device):
        ref, sem = slot
        index = self.slots.setdefault(key, len(self.slots))
        copy = pltpu.make_async_remote_copy(
            src_ref=ref,
            dst_ref=ref,
            send_sem=self.sent.at[index],
            recv_sem=self.recv.at[sem],
            device_id=device,
            device_id_type=MESH,
        )

        @pl.when(cond)
        def _():
            copy.start()

        self.started.append((cond, copy))

    def load(self, cond, source, slot):
        ref, sem = slot

        @pl.when(cond)
        def _():
            pltpu.make_async_copy(source, ref, self.recv.at[sem]).start()

    def arrive(self, cond, slot):
        ref, sem = slot

        @pl.when(cond)
        def _():
            pltpu.make_async_copy(ref, ref, self.recv.at[sem]).wait()

    def finish(self):
        for cond, copy in self.started:

            @pl.when(cond)
            def _():
                copy.wait_send()


RAW_SEM, ROW_SEM, COL_SEM, PIECE_SEM = 0, 16, 28, 44
RECV_SEMS = 76
SEND_SEMS = 128


def kernel(
    mask, cov, out, raw, trail, factor, rows, cols, own, work, left, right, schur, recv, sent,
    own_sem,
):
    r = lax.axis_index("row")
    c = lax.axis_index("col")
    net = Net(recv, sent)
    x, y, z, q = net.x, net.y, net.z, net.q
    both = jnp.logical_and
    always = y >= 0
    top = y == 0
    factors = both(top, z == 0)
    relays = jnp.logical_not(factors)
    own_copy = pltpu.make_async_copy(cov.at[:, 0, :, 0], own, own_sem)
    piece_of = x * 2 + q

    def raw_slot(i, k):
        return raw.at[i, k], RAW_SEM + i * 4 + k

    def row_slot(k, a):
        return rows.at[k, a], ROW_SEM + k * 3 + a

    def col_slot(k, b):
        return cols.at[k, b], COL_SEM + k * 4 + b

    def piece_slot(k, piece):
        span = pl.ds(pl.multiple_of(piece * PIECE, PIECE), PIECE)
        return factor.at[k, pl.ds(0, 4 - k), span], PIECE_SEM + k * 8 + piece

    near = both(factors, x >= q)
    far = both(both(top, z == 1), x >= q + 2)
    net.load(near, cov.at[0, 0, 0, 0], raw_slot(x, q))
    net.load(far, cov.at[0, 0, 0, 0], raw_slot(x, q + 2))
    for b in range(4):
        net.load(top, cov.at[0, 0, b, 0], col_slot(x, b))
    for zs in range(2):
        for a in range(3):
            net.load(z == zs, cov.at[a, 0, 0, 0], row_slot(q + 2 * zs, a))
    own_copy.start()
    net.barrier()

    def send_raw(cond, k, tag):
        slot = raw_slot(x, k)
        net.arrive(cond, slot)
        for n, peer in enumerate(net.group()):
            net.send(cond, ("raw", tag, n), slot, peer)

    def send_rows(cond, zs, a):
        slot = row_slot(q + 2 * zs, a)
        net.arrive(cond, slot)
        rel = (z - zs + NZ) % NZ
        up = rel <= 5
        down = jnp.logical_or(rel == 0, rel >= 8)
        if zs == 1:
            down = both(down, rel != 11)
            net.send(both(cond, rel == 0), ("row", zs, a, 3), slot, net.device(dz=-2))
        net.send(both(cond, up), ("row", zs, a, 0), slot, net.device(dz=1))
        net.send(both(cond, down), ("row", zs, a, 1), slot, net.device(dz=-1))
        net.send(cond, ("row", zs, a, 2), slot, net.device(dq=1))

    def cols_along_y(cond, b):
        slot = col_slot(x, b)
        net.arrive(cond, slot)
        up = y <= 3
        down = jnp.logical_or(y == 0, y >= 6)
        net.send(both(cond, up), ("col", b, 0), slot, net.device(dy=1))
        net.send(both(cond, down), ("col", b, 1), slot, net.device(dy=-1))

    def cols_along_x(cond, b):
        slot = col_slot(x, b)
        for dx in range(1, NX):
            net.send(cond, ("col", b, 1 + dx), slot, net.device(dx=dx))

    send_raw(near, q, 0)
    net.arrive(far, raw_slot(x, q + 2))
    net.send(far, ("raw", 1, 7), raw_slot(x, q + 2), net.device(dz=-1))
    for a in range(3):
        for zs in range(2):
            send_rows(z == zs, zs, a)
        cols_along_y(top, a)
        cols_along_x(both(top, relays), a)
    cols_along_y(top, 3)
    cols_along_x(both(top, relays), 3)
    passed = both(factors, x >= q + 2)
    send_raw(passed, q + 2, 1)

    across = lax.broadcasted_iota(jnp.int32, (128, 128), 1)
    down = lax.broadcasted_iota(jnp.int32, (128, 128), 0)

    def raw_arrive(i, k):
        net.arrive(both(factors, both(jnp.logical_or(x != i, q != k % 2), True)), raw_slot(i, k))

    def subtract(i, j, k):
        old = raw[i, j] if k == 0 else trail[i, j]
        trail[i, j] = old - dot(factor[k, i - k], factor[k, j - k], NT)

    for k in range(LEAD_TILES):
        if k == 0:
            raw_arrive(0, 0)
            for b in range(4):
                cols_along_x(factors, b)

        @pl.when(factors)
        def _():
            work[:, 0:128] = raw[0, 0] if k == 0 else trail[k, k]
            work[:, 128:256] = (across == down).astype(f32)
            for i in range(k + 1, LEAD_TILES):
                for j in range(k, i + 1):
                    if k > 0:
                        subtract(i, j, k - 1)
            factor_tile(work)
            factor[k, 0] = work[:, 128:256]

        if k == 0:
            for i in range(1, LEAD_TILES):
                raw_arrive(i, 0)

        @pl.when(factors)
        def _():
            for i in range(k + 1, LEAD_TILES):
                tile = raw[i, 0] if k == 0 else trail[i, k]
                factor[k, i - k] = dot(tile, work[:, 128:256], NT)

        slot = piece_slot(k, piece_of)
        for n, peer in enumerate(net.ring() + net.column()):
            net.send(factors, ("piece", k, n), slot, peer)
        if k == 0:
            for i in range(1, LEAD_TILES):
                for j in range(1, i + 1):
                    raw_arrive(i, j)

        if k < 3:

            @pl.when(factors)
            def _():
                subtract(k + 1, k + 1, k)

        if k == 0:
            for a in range(3):
                send_rows(factors, 1, a)

    passing = both(relays, top)
    below = jnp.logical_not(top)

    def pass_piece(k):
        slot = piece_slot(k, piece_of)
        net.arrive(relays, slot)
        for n, peer in enumerate(net.column()):
            net.send(passing, ("piece", k, 11 + n), slot, peer)
        for n, peer in enumerate(net.group()):
            net.send(relays, ("piece", k, n), slot, peer)

    def take_pieces(k):
        for n in range(1, 8):
            net.arrive(relays, piece_slot(k, (piece_of + n) % 8))

    def apply_column(k):
        inverse = split(factor[k, 0])
        zk = split(split_dot(inverse, split(right[k])))
        yk = split_dot(split(left[k]), inverse, NT)
        left[k] = yk
        yk = split(yk)
        for i in range(k + 1, LEAD_TILES):
            lower = split(factor[k, i - k])
            right[i] = right[i] - split_dot(lower, zk)
            left[i] = left[i] - split_dot(yk, lower, NT)
        schur[...] = schur[...] - split_dot(yk, zk)

    for b in range(4):
        if b < 3:
            for zs in range(2):
                send_rows(both(relays, z != zs), zs, b)
        cols_along_y(below, b)
        cols_along_x(below, b)
    pass_piece(0)
    own_copy.wait()
    for a in range(3):
        for b in range(4):
            schur[128 * a : 128 * a + 128, 128 * b : 128 * b + 128] = own[a, b] * mask[
                a * 32 + r, b * 24 + c
            ].astype(f32)
    for dx in range(1, NX):
        for b in range(4):
            net.arrive(always, col_slot((x + dx) % NX, b))
    for k in range(LEAD_TILES):
        for b in range(4):
            right[k, :, 128 * b : 128 * b + 128] = cols[k, b] * mask[k, b * 24 + c].astype(f32)
    pass_piece(1)
    for zs in range(2):
        for a in range(3):
            net.arrive(always, row_slot(1 - q + 2 * zs, a))
    for k in range(LEAD_TILES):
        for a in range(3):
            left[k, 128 * a : 128 * a + 128, :] = rows[k, a] * mask[a * 32 + r, k].astype(f32)
    take_pieces(0)
    apply_column(0)
    pass_piece(2)
    take_pieces(1)
    apply_column(1)
    pass_piece(3)
    take_pieces(2)
    apply_column(2)
    take_pieces(3)
    apply_column(3)

    edge = jnp.minimum(c, 3)
    for a in range(3):
        tile_row = a * 32 + r
        for b in range(4):
            value = schur[128 * a : 128 * a + 128, 128 * b : 128 * b + 128]
            if a == 0:
                value = jnp.where(r < LEAD_TILES, 0.0, value)
            if b == 0:
                lower = (tile_row - c) * 128 + down >= across
                column = jnp.where(lower, left[edge, 128 * a : 128 * a + 128, :], 0.0)
                value = jnp.where(c < LEAD_TILES, column, value)
            out[a, 0, b, 0] = value.astype(jnp.bfloat16)
    net.finish()


def on_device(covariance, tile_mask):
    vmem = pltpu.VMEM
    return pl.pallas_call(
        kernel,
        out_shape=jax.ShapeDtypeStruct(covariance.shape, jnp.bfloat16),
        in_specs=[pl.BlockSpec(memory_space=pltpu.SMEM), pl.BlockSpec(memory_space=pl.ANY)],
        out_specs=pl.BlockSpec(memory_space=vmem),
        scratch_shapes=[
            vmem((4, 4, 128, 128), f32),
            vmem((4, 4, 128, 128), f32),
            vmem((4, 4, 128, 128), f32),
            vmem((4, 3, 128, 128), f32),
            vmem((4, 4, 128, 128), f32),
            vmem((3, 4, 128, 128), f32),
            vmem((128, 256), f32),
            vmem((4, 384, 128), f32),
            vmem((4, 128, 512), f32),
            vmem((384, 512), f32),
            pltpu.SemaphoreType.DMA((RECV_SEMS,)),
            pltpu.SemaphoreType.DMA((SEND_SEMS,)),
            pltpu.SemaphoreType.DMA,
        ],
        compiler_params=pltpu.CompilerParams(collective_id=0, has_side_effects=True),
        name="panels",
    )(tile_mask, covariance)


def solution(mesh):
    in_specs = (P(None, "row", None, "col", None, None), P())
    out_specs = P(None, "row", None, "col", None, None)
    return jax.shard_map(
        on_device, mesh=mesh, in_specs=in_specs, out_specs=out_specs, check_vma=False
    )
```

```python
import functools

import jax
import jax.numpy as jnp
from jax import lax
from jax.experimental import pallas as pl
from jax.experimental.pallas import tpu as pltpu
from jax.sharding import PartitionSpec as P

MESH = pl.DeviceIdType.MESH
f32 = jnp.float32
NN = (((1,), (0,)), ((), ()))
NT = (((1,), (1,)), ((), ()))
TN = (((0,), (0,)), ((), ()))
NX = 4
NY = 8
NZ = 12
LEAD_TILES = 4
PIECE = 16


def dot(a, b, dims=NN):
    return lax.dot_general(
        a, b, dims, precision=lax.Precision.HIGHEST, preferred_element_type=f32
    )


def factor_tile(work):
    sub = lax.broadcasted_iota(jnp.int32, (8, 128), 0)

    def across(value, k):
        return jnp.broadcast_to(value[k : k + 1, :], (8, 128))

    def along(value, k):
        return jnp.broadcast_to(value[:, k : k + 1], (8, 128))

    for group in range(4):
        q0 = 32 * group
        xa = [work[q0 + 8 * i : q0 + 8 * i + 8, 0:128] for i in range(4)]
        xe = [work[q0 + 8 * i : q0 + 8 * i + 8, 128:256] for i in range(4)]
        for block in range(4):
            live = range(block, 4)
            heads = {i: [along(xa[i], q0 + 8 * block + k) for k in range(8)] for i in live}
            pivots = jnp.ones((8, 128), f32)
            for k in range(8):
                pivot = across(heads[block][k], k)
                inverse = 1.0 / pivot
                ra = across(xa[block], k)
                re = across(xe[block], k)
                pivots = jnp.where(sub == k, pivot, pivots)
                m = {i: heads[i][k] * inverse for i in live}
                m[block] = jnp.where(sub > k, m[block], 0.0)
                for j in range(k + 1, 8):
                    entry = across(heads[block][j], k)
                    for i in live:
                        heads[i][j] = heads[i][j] - m[i] * entry
                for i in live:
                    xa[i] = xa[i] - m[i] * ra
                    xe[i] = xe[i] - m[i] * re
            scale = lax.rsqrt(pivots)
            xa[block] = xa[block] * scale
            xe[block] = xe[block] * scale
            r0 = q0 + 8 * block
            work[r0 : r0 + 8, 0:128] = xa[block]
            work[r0 : r0 + 8, 128:256] = xe[block]
        if group < 3:
            upper = jnp.concatenate(xa, axis=0)
            both = jnp.concatenate([upper, jnp.concatenate(xe, axis=0)], axis=1)
            turned = upper.T
            q1, q2 = q0 + 32, q0 + 64
            work[q1:q2, :] = work[q1:q2, :] - dot(turned[q1:q2, :], both)
            if group < 2:
                work[q2:, :] = work[q2:, :] - dot(turned[q2:, :], both)


def split(value):
    high = value.astype(jnp.bfloat16)
    return high, (value - high.astype(f32)).astype(jnp.bfloat16)


def split_dot(a, b, dims=NN):
    def part(i, j):
        return lax.dot_general(a[i], b[j], dims, preferred_element_type=f32)

    return part(0, 0) + (part(0, 1) + part(1, 0))


class Net:
    def __init__(self, recv, sent):
        self.recv, self.sent = recv, sent
        row = lax.axis_index("row")
        col = lax.axis_index("col")
        self.y, self.x = row // NX, row % NX
        self.z, self.q = col // 2, col % 2
        self.started = []
        self.slots = {}
        self.arrivals = {}

    def device(self, dx=0, dy=0, dz=0, dq=0):
        x = (self.x + dx) % NX
        y = (self.y + dy + NY) % NY
        z = (self.z + dz + NZ) % NZ
        q = (self.q + dq) % 2
        return (y * NX + x, z * 2 + q)

    def group(self):
        return [
            self.device(dx=dx, dq=dq) for dx in (2, 1, 3, 0) for dq in (0, 1) if dx or dq
        ]

    def column(self):
        return [self.device(dy=dy) for dy in (4, 3, -3, 2, -2, 1, -1)]

    def ring(self):
        return [self.device(dz=dz) for dz in (6, 5, -5, 4, -4, 3, -3, 2, -2, 1, -1)]

    def barrier(self):
        sem = pltpu.get_barrier_semaphore()
        peers = self.ring() + self.column() + self.group()
        for peer in peers:
            pl.semaphore_signal(sem, inc=1, device_id=peer, device_id_type=MESH)
        pl.semaphore_wait(sem, len(peers))

    def send(self, cond, key, slot, device):
        ref, sem = slot
        index = self.slots.setdefault(key, len(self.slots))
        copy = pltpu.make_async_remote_copy(
            src_ref=ref,
            dst_ref=ref,
            send_sem=self.sent.at[index],
            recv_sem=self.recv.at[sem],
            device_id=device,
            device_id_type=MESH,
        )

        @pl.when(cond)
        def _():
            copy.start()

        self.started.append((cond, copy))

    def load(self, cond, source, slot):
        ref, sem = slot

        @pl.when(cond)
        def _():
            pltpu.make_async_copy(source, ref, self.recv.at[sem]).start()

    def arrive(self, cond, slot):
        ref, sem = slot

        @pl.when(cond)
        def _():
            pltpu.make_async_copy(ref, ref, self.recv.at[sem]).wait()

    def finish(self):
        for cond, copy in self.started:

            @pl.when(cond)
            def _():
                copy.wait_send()


RAW_SEM, ROW_SEM, COL_SEM, PIECE_SEM = 0, 16, 28, 44
RECV_SEMS = 76
SEND_SEMS = 128


def kernel(
    mask, cov, out, raw, trail, factor, rows, cols, own, work, left, right, schur, recv, sent,
    own_sem,
):
    r = lax.axis_index("row")
    c = lax.axis_index("col")
    net = Net(recv, sent)
    x, y, z, q = net.x, net.y, net.z, net.q
    both = jnp.logical_and
    always = y >= 0
    top = y == 0
    factors = both(top, z == 0)
    relays = jnp.logical_not(factors)
    own_copy = pltpu.make_async_copy(cov.at[:, 0, :, 0], own, own_sem)
    piece_of = x * 2 + q

    def raw_slot(i, k):
        return raw.at[i, k], RAW_SEM + i * 4 + k

    def row_slot(k, a):
        return rows.at[k, a], ROW_SEM + k * 3 + a

    def col_slot(k, b):
        return cols.at[k, b], COL_SEM + k * 4 + b

    def piece_slot(k, piece):
        span = pl.ds(pl.multiple_of(piece * PIECE, PIECE), PIECE)
        return factor.at[k, pl.ds(0, 4 - k), span], PIECE_SEM + k * 8 + piece

    near = both(factors, x >= q)
    far = both(both(top, z == 1), x >= q + 2)
    net.load(near, cov.at[0, 0, 0, 0], raw_slot(x, q))
    net.load(far, cov.at[0, 0, 0, 0], raw_slot(x, q + 2))
    for b in range(4):
        net.load(top, cov.at[0, 0, b, 0], col_slot(x, b))
    for zs in range(2):
        for a in range(3):
            net.load(z == zs, cov.at[a, 0, 0, 0], row_slot(q + 2 * zs, a))
    own_copy.start()
    net.barrier()

    def send_raw(cond, k, tag):
        slot = raw_slot(x, k)
        net.arrive(cond, slot)
        for n, peer in enumerate(net.group()):
            net.send(cond, ("raw", tag, n), slot, peer)

    def send_rows(cond, zs, a):
        slot = row_slot(q + 2 * zs, a)
        net.arrive(cond, slot)
        rel = (z - zs + NZ) % NZ
        up = rel <= 5
        down = jnp.logical_or(rel == 0, rel >= 8)
        if zs == 1:
            down = both(down, rel != 11)
            net.send(both(cond, rel == 0), ("row", zs, a, 3), slot, net.device(dz=-2))
        net.send(both(cond, up), ("row", zs, a, 0), slot, net.device(dz=1))
        net.send(both(cond, down), ("row", zs, a, 1), slot, net.device(dz=-1))
        net.send(cond, ("row", zs, a, 2), slot, net.device(dq=1))

    def cols_along_y(cond, b):
        slot = col_slot(x, b)
        net.arrive(cond, slot)
        up = y <= 3
        down = jnp.logical_or(y == 0, y >= 6)
        net.send(both(cond, up), ("col", b, 0), slot, net.device(dy=1))
        net.send(both(cond, down), ("col", b, 1), slot, net.device(dy=-1))

    def cols_along_x(cond, b):
        slot = col_slot(x, b)
        for dx in range(1, NX):
            net.send(cond, ("col", b, 1 + dx), slot, net.device(dx=dx))

    send_raw(near, q, 0)
    net.arrive(far, raw_slot(x, q + 2))
    net.send(far, ("raw", 1, 7), raw_slot(x, q + 2), net.device(dz=-1))
    for a in range(3):
        for zs in range(2):
            send_rows(z == zs, zs, a)
        cols_along_y(top, a)
        cols_along_x(both(top, relays), a)
    cols_along_y(top, 3)
    cols_along_x(both(top, relays), 3)
    passed = both(factors, x >= q + 2)
    send_raw(passed, q + 2, 1)

    across = lax.broadcasted_iota(jnp.int32, (128, 128), 1)
    down = lax.broadcasted_iota(jnp.int32, (128, 128), 0)

    def raw_arrive(i, k):
        net.arrive(both(factors, both(jnp.logical_or(x != i, q != k % 2), True)), raw_slot(i, k))

    def subtract(i, j, k):
        old = raw[i, j] if k == 0 else trail[i, j]
        trail[i, j] = old - dot(factor[k, i - k], factor[k, j - k], NT)

    for k in range(LEAD_TILES):
        if k == 0:
            raw_arrive(0, 0)
            for b in range(4):
                cols_along_x(factors, b)

        @pl.when(factors)
        def _():
            work[:, 0:128] = raw[0, 0] if k == 0 else trail[k, k]
            work[:, 128:256] = (across == down).astype(f32)
            for i in range(k + 1, LEAD_TILES):
                for j in range(k, i + 1):
                    if k > 0:
                        subtract(i, j, k - 1)
            factor_tile(work)
            factor[k, 0] = work[:, 128:256]

        if k == 0:
            for i in range(1, LEAD_TILES):
                raw_arrive(i, 0)

        @pl.when(factors)
        def _():
            for i in range(k + 1, LEAD_TILES):
                tile = raw[i, 0] if k == 0 else trail[i, k]
                factor[k, i - k] = dot(tile, work[:, 128:256], NT)

        slot = piece_slot(k, piece_of)
        for n, peer in enumerate(net.ring() + net.column()):
            net.send(factors, ("piece", k, n), slot, peer)
        if k == 0:
            for i in range(1, LEAD_TILES):
                for j in range(1, i + 1):
                    raw_arrive(i, j)

        if k < 3:

            @pl.when(factors)
            def _():
                subtract(k + 1, k + 1, k)

        if k == 0:
            for a in range(3):
                send_rows(factors, 1, a)

    passing = both(relays, top)
    below = jnp.logical_not(top)

    def pass_piece(k, cond):
        slot = piece_slot(k, piece_of)
        net.arrive(cond, slot)
        for n, peer in enumerate(net.column()):
            net.send(both(cond, top), ("piece", k, 11 + n), slot, peer)
        for n, peer in enumerate(net.group()):
            net.send(cond, ("piece", k, n), slot, peer)

    def take_pieces(k):
        for n in range(1, 8):
            net.arrive(relays, piece_slot(k, (piece_of + n) % 8))

    def apply_column(k):
        inverse = split(factor[k, 0])
        zk = split(split_dot(inverse, split(right[k])))
        yk = split_dot(split(left[k]), inverse, NT)
        left[k] = yk
        yk = split(yk)
        for i in range(k + 1, LEAD_TILES):
            lower = split(factor[k, i - k])
            right[i] = right[i] - split_dot(lower, zk)
            left[i] = left[i] - split_dot(yk, lower, NT)
        schur[...] = schur[...] - split_dot(yk, zk)

    z_hops = jnp.where(z <= 6, z, NZ + 1 - z)
    y_hops = jnp.minimum(y, NY - y)

    def relay_rows(cond):
        for a in range(3):
            for zs in range(2):
                send_rows(both(both(relays, z != zs), cond), zs, a)

    relay_rows(z_hops <= y_hops)
    for b in range(4):
        cols_along_y(below, b)
        cols_along_x(below, b)
    relay_rows(z_hops > y_hops)
    pass_piece(0, relays)
    own_copy.wait()
    for a in range(3):
        for b in range(4):
            schur[128 * a : 128 * a + 128, 128 * b : 128 * b + 128] = own[a, b] * mask[
                a * 32 + r, b * 24 + c
            ].astype(f32)
    for dx in range(1, NX):
        for b in range(4):
            net.arrive(always, col_slot((x + dx) % NX, b))
    for k in range(LEAD_TILES):
        for b in range(4):
            right[k, :, 128 * b : 128 * b + 128] = cols[k, b] * mask[k, b * 24 + c].astype(f32)
    pass_piece(1, relays)
    for zs in range(2):
        for a in range(3):
            net.arrive(always, row_slot(1 - q + 2 * zs, a))
    for k in range(LEAD_TILES):
        for a in range(3):
            left[k, 128 * a : 128 * a + 128, :] = rows[k, a] * mask[a * 32 + r, k].astype(f32)
    pass_piece(2, passing)
    pass_piece(3, passing)
    take_pieces(0)
    apply_column(0)
    pass_piece(2, below)
    take_pieces(1)
    apply_column(1)
    pass_piece(3, below)
    take_pieces(2)
    apply_column(2)
    take_pieces(3)
    apply_column(3)

    edge = jnp.minimum(c, 3)
    for a in range(3):
        tile_row = a * 32 + r
        for b in range(4):
            value = schur[128 * a : 128 * a + 128, 128 * b : 128 * b + 128]
            if a == 0:
                value = jnp.where(r < LEAD_TILES, 0.0, value)
            if b == 0:
                lower = (tile_row - c) * 128 + down >= across
                column = jnp.where(lower, left[edge, 128 * a : 128 * a + 128, :], 0.0)
                value = jnp.where(c < LEAD_TILES, column, value)
            out[a, 0, b, 0] = value.astype(jnp.bfloat16)
    net.finish()


def on_device(covariance, tile_mask):
    vmem = pltpu.VMEM
    return pl.pallas_call(
        kernel,
        out_shape=jax.ShapeDtypeStruct(covariance.shape, jnp.bfloat16),
        in_specs=[pl.BlockSpec(memory_space=pltpu.SMEM), pl.BlockSpec(memory_space=pl.ANY)],
        out_specs=pl.BlockSpec(memory_space=vmem),
        scratch_shapes=[
            vmem((4, 4, 128, 128), f32),
            vmem((4, 4, 128, 128), f32),
            vmem((4, 4, 128, 128), f32),
            vmem((4, 3, 128, 128), f32),
            vmem((4, 4, 128, 128), f32),
            vmem((3, 4, 128, 128), f32),
            vmem((128, 256), f32),
            vmem((4, 384, 128), f32),
            vmem((4, 128, 512), f32),
            vmem((384, 512), f32),
            pltpu.SemaphoreType.DMA((RECV_SEMS,)),
            pltpu.SemaphoreType.DMA((SEND_SEMS,)),
            pltpu.SemaphoreType.DMA,
        ],
        compiler_params=pltpu.CompilerParams(collective_id=0, has_side_effects=True),
        name="panels",
    )(tile_mask, covariance)


def solution(mesh):
    in_specs = (P(None, "row", None, "col", None, None), P())
    out_specs = P(None, "row", None, "col", None, None)
    return jax.shard_map(
        on_device, mesh=mesh, in_specs=in_specs, out_specs=out_specs, check_vma=False
    )
```

```python
import functools

import jax
import jax.numpy as jnp
from jax import lax
from jax.experimental import pallas as pl
from jax.experimental.pallas import tpu as pltpu
from jax.sharding import PartitionSpec as P

MESH = pl.DeviceIdType.MESH
f32 = jnp.float32
NN = (((1,), (0,)), ((), ()))
NT = (((1,), (1,)), ((), ()))
TN = (((0,), (0,)), ((), ()))
NX = 4
NY = 8
NZ = 12
LEAD_TILES = 4
PIECE = 16


def dot(a, b, dims=NN):
    return lax.dot_general(
        a, b, dims, precision=lax.Precision.HIGHEST, preferred_element_type=f32
    )


def factor_tile(work):
    sub = lax.broadcasted_iota(jnp.int32, (8, 128), 0)

    def across(value, k):
        return jnp.broadcast_to(value[k : k + 1, :], (8, 128))

    def along(value, k):
        return jnp.broadcast_to(value[:, k : k + 1], (8, 128))

    for group in range(4):
        q0 = 32 * group
        xa = [work[q0 + 8 * i : q0 + 8 * i + 8, 0:128] for i in range(4)]
        xe = [work[q0 + 8 * i : q0 + 8 * i + 8, 128:256] for i in range(4)]
        for block in range(4):
            live = range(block, 4)
            heads = {i: [along(xa[i], q0 + 8 * block + k) for k in range(8)] for i in live}
            pivots = jnp.ones((8, 128), f32)
            for k in range(8):
                pivot = across(heads[block][k], k)
                inverse = 1.0 / pivot
                ra = across(xa[block], k)
                re = across(xe[block], k)
                pivots = jnp.where(sub == k, pivot, pivots)
                m = {i: heads[i][k] * inverse for i in live}
                m[block] = jnp.where(sub > k, m[block], 0.0)
                for j in range(k + 1, 8):
                    entry = across(heads[block][j], k)
                    for i in live:
                        heads[i][j] = heads[i][j] - m[i] * entry
                for i in live:
                    xa[i] = xa[i] - m[i] * ra
                    xe[i] = xe[i] - m[i] * re
            scale = lax.rsqrt(pivots)
            xa[block] = xa[block] * scale
            xe[block] = xe[block] * scale
            r0 = q0 + 8 * block
            work[r0 : r0 + 8, 0:128] = xa[block]
            work[r0 : r0 + 8, 128:256] = xe[block]
        if group < 3:
            upper = jnp.concatenate(xa, axis=0)
            both = jnp.concatenate([upper, jnp.concatenate(xe, axis=0)], axis=1)
            turned = upper.T
            q1, q2 = q0 + 32, q0 + 64
            work[q1:q2, :] = work[q1:q2, :] - dot(turned[q1:q2, :], both)
            if group < 2:
                work[q2:, :] = work[q2:, :] - dot(turned[q2:, :], both)


def split(value):
    high = value.astype(jnp.bfloat16)
    return high, (value - high.astype(f32)).astype(jnp.bfloat16)


def split_dot(a, b, dims=NN):
    def part(i, j):
        return lax.dot_general(a[i], b[j], dims, preferred_element_type=f32)

    return part(0, 0) + (part(0, 1) + part(1, 0))


class Net:
    def __init__(self, recv, sent):
        self.recv, self.sent = recv, sent
        row = lax.axis_index("row")
        col = lax.axis_index("col")
        self.y, self.x = row // NX, row % NX
        self.z, self.q = col // 2, col % 2
        self.started = []
        self.slots = {}
        self.arrivals = {}

    def device(self, dx=0, dy=0, dz=0, dq=0):
        x = (self.x + dx) % NX
        y = (self.y + dy + NY) % NY
        z = (self.z + dz + NZ) % NZ
        q = (self.q + dq) % 2
        return (y * NX + x, z * 2 + q)

    def group(self):
        return [
            self.device(dx=dx, dq=dq) for dx in (2, 1, 3, 0) for dq in (0, 1) if dx or dq
        ]

    def column(self):
        return [self.device(dy=dy) for dy in (4, 3, -3, 2, -2, 1, -1)]

    def ring(self):
        return [self.device(dz=dz) for dz in (6, 5, -5, 4, -4, 3, -3, 2, -2, 1, -1)]

    def barrier(self):
        sem = pltpu.get_barrier_semaphore()
        peers = self.ring() + self.column() + self.group()
        for peer in peers:
            pl.semaphore_signal(sem, inc=1, device_id=peer, device_id_type=MESH)
        pl.semaphore_wait(sem, len(peers))

    def send(self, cond, key, slot, device, later=False):
        ref, sem = slot
        index = self.slots.setdefault(key, len(self.slots))
        copy = pltpu.make_async_remote_copy(
            src_ref=ref,
            dst_ref=ref,
            send_sem=self.sent.at[index],
            recv_sem=self.recv.at[sem],
            device_id=device,
            device_id_type=MESH,
        )

        if not later:

            @pl.when(cond)
            def _():
                copy.start()

        self.started.append((cond, copy))
        return copy

    def load(self, cond, source, slot):
        ref, sem = slot

        @pl.when(cond)
        def _():
            pltpu.make_async_copy(source, ref, self.recv.at[sem]).start()

    def arrive(self, cond, slot):
        ref, sem = slot

        @pl.when(cond)
        def _():
            pltpu.make_async_copy(ref, ref, self.recv.at[sem]).wait()

    def finish(self):
        for cond, copy in self.started:

            @pl.when(cond)
            def _():
                copy.wait_send()


RAW_SEM, ROW_SEM, COL_SEM, PIECE_SEM = 0, 16, 28, 44
RECV_SEMS = 76
SEND_SEMS = 128


def kernel(
    mask, cov, out, raw, trail, factor, rows, cols, own, work, left, right, schur, recv, sent,
    own_sem,
):
    r = lax.axis_index("row")
    c = lax.axis_index("col")
    net = Net(recv, sent)
    x, y, z, q = net.x, net.y, net.z, net.q
    both = jnp.logical_and
    always = y >= 0
    top = y == 0
    factors = both(top, z == 0)
    relays = jnp.logical_not(factors)
    own_copy = pltpu.make_async_copy(cov.at[:, 0, :, 0], own, own_sem)
    piece_of = x * 2 + q

    def raw_slot(i, k):
        return raw.at[i, k], RAW_SEM + i * 4 + k

    def row_slot(k, a):
        return rows.at[k, a], ROW_SEM + k * 3 + a

    def col_slot(k, b):
        return cols.at[k, b], COL_SEM + k * 4 + b

    def piece_slot(k, piece):
        span = pl.ds(pl.multiple_of(piece * PIECE, PIECE), PIECE)
        return factor.at[k, pl.ds(0, 4 - k), span], PIECE_SEM + k * 8 + piece

    near = both(factors, x >= q)
    far = both(both(top, z == 1), x >= q + 2)
    net.load(near, cov.at[0, 0, 0, 0], raw_slot(x, q))
    net.load(far, cov.at[0, 0, 0, 0], raw_slot(x, q + 2))
    for b in range(4):
        net.load(top, cov.at[0, 0, b, 0], col_slot(x, b))
    for zs in range(2):
        for a in range(3):
            net.load(z == zs, cov.at[a, 0, 0, 0], row_slot(q + 2 * zs, a))
    own_copy.start()
    net.barrier()

    def send_raw(cond, k, tag):
        slot = raw_slot(x, k)
        net.arrive(cond, slot)
        for n, peer in enumerate(net.group()):
            net.send(cond, ("raw", tag, n), slot, peer)

    def send_rows(cond, zs, a):
        slot = row_slot(q + 2 * zs, a)
        net.arrive(cond, slot)
        rel = (z - zs + NZ) % NZ
        up = rel <= 5
        down = jnp.logical_or(rel == 0, rel >= 8)
        if zs == 1:
            down = both(down, rel != 11)
            net.send(both(cond, rel == 0), ("row", zs, a, 3), slot, net.device(dz=-2))
        net.send(both(cond, up), ("row", zs, a, 0), slot, net.device(dz=1))
        net.send(both(cond, down), ("row", zs, a, 1), slot, net.device(dz=-1))
        net.send(cond, ("row", zs, a, 2), slot, net.device(dq=1))

    def cols_along_y(cond, b):
        slot = col_slot(x, b)
        net.arrive(cond, slot)
        up = y <= 3
        down = jnp.logical_or(y == 0, y >= 6)
        net.send(both(cond, up), ("col", b, 0), slot, net.device(dy=1))
        net.send(both(cond, down), ("col", b, 1), slot, net.device(dy=-1))

    def cols_along_x(cond, b, later=False):
        slot = col_slot(x, b)
        return [
            net.send(cond, ("col", b, 1 + dx), slot, net.device(dx=dx), later)
            for dx in range(1, NX)
        ]

    send_raw(near, q, 0)
    net.arrive(far, raw_slot(x, q + 2))
    net.send(far, ("raw", 1, 7), raw_slot(x, q + 2), net.device(dz=-1))
    for a in range(3):
        for zs in range(2):
            send_rows(z == zs, zs, a)
        cols_along_y(top, a)
        cols_along_x(both(top, relays), a)
    cols_along_y(top, 3)
    cols_along_x(both(top, relays), 3)
    passed = both(factors, x >= q + 2)
    send_raw(passed, q + 2, 1)

    across = lax.broadcasted_iota(jnp.int32, (128, 128), 1)
    down = lax.broadcasted_iota(jnp.int32, (128, 128), 0)

    def raw_arrive(i, k):
        net.arrive(both(factors, both(jnp.logical_or(x != i, q != k % 2), True)), raw_slot(i, k))

    def piece_copies(k):
        slot = piece_slot(k, piece_of)
        return [
            net.send(factors, ("piece", k, n), slot, peer, later=True)
            for n, peer in enumerate(net.column() + net.ring())
        ]

    def subtract(i, j, k):
        old = raw[i, j] if k == 0 else trail[i, j]
        trail[i, j] = old - dot(factor[k, i - k], factor[k, j - k], NT)

    for k in range(LEAD_TILES):
        if k == 0:
            raw_arrive(0, 0)
            held = [copy for b in range(4) for copy in cols_along_x(factors, b, later=True)]
        else:
            held = piece_copies(k - 1)

        @pl.when(factors)
        def _():
            work[:, 0:128] = raw[0, 0] if k == 0 else trail[k, k]
            work[:, 128:256] = (across == down).astype(f32)
            for i in range(k + 1, LEAD_TILES):
                for j in range(k, i + 1):
                    if k > 0:
                        subtract(i, j, k - 1)
            for copy in held:
                copy.start()
            factor_tile(work)
            factor[k, 0] = work[:, 128:256]

        if k == 0:
            for i in range(1, LEAD_TILES):
                raw_arrive(i, 0)

        @pl.when(factors)
        def _():
            for i in range(k + 1, LEAD_TILES):
                tile = raw[i, 0] if k == 0 else trail[i, k]
                factor[k, i - k] = dot(tile, work[:, 128:256], NT)

        if k == 3:

            held = piece_copies(3)

            @pl.when(factors)
            def _():
                for copy in held:
                    copy.start()

        if k == 0:
            for i in range(1, LEAD_TILES):
                for j in range(1, i + 1):
                    raw_arrive(i, j)

        if k < 3:

            @pl.when(factors)
            def _():
                subtract(k + 1, k + 1, k)

    for a in range(3):
        send_rows(factors, 1, a)

    passing = both(relays, top)
    below = jnp.logical_not(top)

    def pass_piece(k, cond):
        slot = piece_slot(k, piece_of)
        net.arrive(cond, slot)
        for n, peer in enumerate(net.column()):
            net.send(both(cond, top), ("piece", k, 11 + n), slot, peer)
        for n, peer in enumerate(net.group()):
            net.send(cond, ("piece", k, n), slot, peer)

    def take_pieces(k):
        for n in range(1, 8):
            net.arrive(relays, piece_slot(k, (piece_of + n) % 8))

    def apply_column(k):
        inverse = split(factor[k, 0])
        zk = split(split_dot(inverse, split(right[k])))
        yk = split_dot(split(left[k]), inverse, NT)
        left[k] = yk
        yk = split(yk)
        for i in range(k + 1, LEAD_TILES):
            lower = split(factor[k, i - k])
            right[i] = right[i] - split_dot(lower, zk)
            left[i] = left[i] - split_dot(yk, lower, NT)
        schur[...] = schur[...] - split_dot(yk, zk)

    z_hops = jnp.where(z <= 6, z, NZ + 1 - z)
    y_hops = jnp.minimum(y, NY - y)

    def relay_rows(cond):
        for a in range(3):
            for zs in range(2):
                send_rows(both(both(relays, z != zs), cond), zs, a)

    relay_rows(z_hops <= y_hops)
    for b in range(4):
        cols_along_y(below, b)
        cols_along_x(below, b)
    relay_rows(z_hops > y_hops)
    pass_piece(0, relays)
    own_copy.wait()
    for a in range(3):
        for b in range(4):
            schur[128 * a : 128 * a + 128, 128 * b : 128 * b + 128] = own[a, b] * mask[
                a * 32 + r, b * 24 + c
            ].astype(f32)
    for dx in range(1, NX):
        for b in range(4):
            net.arrive(always, col_slot((x + dx) % NX, b))
    for k in range(LEAD_TILES):
        for b in range(4):
            right[k, :, 128 * b : 128 * b + 128] = cols[k, b] * mask[k, b * 24 + c].astype(f32)
    pass_piece(1, relays)
    for zs in range(2):
        for a in range(3):
            net.arrive(always, row_slot(1 - q + 2 * zs, a))
    for k in range(LEAD_TILES):
        for a in range(3):
            left[k, 128 * a : 128 * a + 128, :] = rows[k, a] * mask[a * 32 + r, k].astype(f32)
    pass_piece(2, passing)
    pass_piece(3, passing)
    take_pieces(0)
    apply_column(0)
    pass_piece(2, below)
    take_pieces(1)
    apply_column(1)
    pass_piece(3, below)
    take_pieces(2)
    apply_column(2)
    take_pieces(3)
    apply_column(3)

    edge = jnp.minimum(c, 3)
    for a in range(3):
        tile_row = a * 32 + r
        for b in range(4):
            value = schur[128 * a : 128 * a + 128, 128 * b : 128 * b + 128]
            if a == 0:
                value = jnp.where(r < LEAD_TILES, 0.0, value)
            if b == 0:
                lower = (tile_row - c) * 128 + down >= across
                column = jnp.where(lower, left[edge, 128 * a : 128 * a + 128, :], 0.0)
                value = jnp.where(c < LEAD_TILES, column, value)
            out[a, 0, b, 0] = value.astype(jnp.bfloat16)
    net.finish()


def on_device(covariance, tile_mask):
    vmem = pltpu.VMEM
    return pl.pallas_call(
        kernel,
        out_shape=jax.ShapeDtypeStruct(covariance.shape, jnp.bfloat16),
        in_specs=[pl.BlockSpec(memory_space=pltpu.SMEM), pl.BlockSpec(memory_space=pl.ANY)],
        out_specs=pl.BlockSpec(memory_space=vmem),
        scratch_shapes=[
            vmem((4, 4, 128, 128), f32),
            vmem((4, 4, 128, 128), f32),
            vmem((4, 4, 128, 128), f32),
            vmem((4, 3, 128, 128), f32),
            vmem((4, 4, 128, 128), f32),
            vmem((3, 4, 128, 128), f32),
            vmem((128, 256), f32),
            vmem((4, 384, 128), f32),
            vmem((4, 128, 512), f32),
            vmem((384, 512), f32),
            pltpu.SemaphoreType.DMA((RECV_SEMS,)),
            pltpu.SemaphoreType.DMA((SEND_SEMS,)),
            pltpu.SemaphoreType.DMA,
        ],
        compiler_params=pltpu.CompilerParams(collective_id=0, has_side_effects=True),
        name="panels",
    )(tile_mask, covariance)


def solution(mesh):
    in_specs = (P(None, "row", None, "col", None, None), P())
    out_specs = P(None, "row", None, "col", None, None)
    return jax.shard_map(
        on_device, mesh=mesh, in_specs=in_specs, out_specs=out_specs, check_vma=False
    )
```
